32 devices in a mesh: row: 8 (over y, x, core), col: 4 (over z).
Axes of the slice: x: 2, y: 2, z: 4, core: 2. Of those that a mesh axis runs over, the one named last changes fastest.
Arguments:
- amplitudes: float32 [512, 32, 32, 32], P('col', 'row'), may hold values from -6 to 6
- integrals: float32 [1024, 16384], P('col', 'row'), may hold values from -0.1875 to 0.1875
- occ_energy: float32 [32], replicated, may hold values from -2 to -0.5
- vir_energy: float32 [512], replicated, may hold values from 0.3 to 3
Outputs:
- residual: float32 [16384, 16384], P('col', 'row')
The draws below stay inside these ranges and needn't reach their ends.
All inputs are finite; a program needn't handle non-finite values.
Results may differ from the reference program's by a relative error of at most 0.00007.
Values sent between devices are 32-bit elements; how exact they have to be, the bound alone decides.
A program may use at most 192 MiB of HBM per device.

```python
import jax
import jax.numpy as jnp
from jax import lax

V = 512
O = 32
KWIN = 1024
NOV = 16384
CWIN = 32


def block_scale(own_key, shape, cuts, least, high):
    factor_of = 1.0
    for dim, parts in cuts:
        steps = jax.random.uniform(jax.random.fold_in(jax.random.fold_in(own_key, 6), dim), (parts,), jnp.float32, least / len(cuts), high / len(cuts))
        factor_of = factor_of * jnp.repeat(jnp.exp(steps), shape[dim] // parts).reshape((-1,) + (1,) * (len(shape) - 1 - dim))
    return factor_of


def gaussian(key, dims, spread, most, cuts=(), dtype=jnp.bfloat16):
    result = spread * jax.random.normal(key, dims, jnp.float32)
    if cuts:
        result = result * block_scale(key, dims, cuts, -0.22, 0.18)
    return jnp.clip(result, -most, most).astype(dtype)


def setup_inputs(seed: int = 0) -> dict:
    arg_keys = jax.random.split(jax.random.key(seed), 5)
    amplitudes = gaussian(arg_keys[0], (V, O, CWIN, O), 1.0, 6.0, ((0, 4), (1, 8)), jnp.float32)
    integrals = gaussian(arg_keys[1], (KWIN, NOV), KWIN ** -0.5, 0.1875, ((0, 4), (1, 8)), jnp.float32)
    occ_energy = jnp.clip(jax.random.uniform(arg_keys[2], (O,), jnp.float32, -2.0, -0.5), -2.0, -0.5)
    vir_energy = jnp.clip(jax.random.uniform(arg_keys[3], (V,), jnp.float32, 0.3, 3.0), 0.3, 3.0)
    return {"amplitudes": amplitudes, "integrals": integrals, "occ_energy": occ_energy, "vir_energy": vir_energy}


def reference(amplitudes, integrals, occ_energy, vir_energy):
    amp_matrix = amplitudes.reshape(V * O, KWIN)
    contracted = jnp.dot(amp_matrix, integrals, preferred_element_type=jnp.float32, precision=lax.Precision.HIGHEST)
    gap = (vir_energy[:, None] - occ_energy[None, :]).reshape(V * O)
    return contracted / (gap[:, None] + gap[None, :])
```

```python
import jax
import jax.numpy as jnp
from jax import lax
from jax.experimental import pallas as pl
from jax.experimental.pallas import tpu as pltpu
from jax.sharding import PartitionSpec as P

CUTS = (0, 1, 2, 4)


def flip_kernel(x_ref, o_ref):
    o_ref[0] = jnp.swapaxes(x_ref[0], 0, 1)


def flip(x):
    own, depth, virtuals = x.shape
    return pl.pallas_call(
        flip_kernel,
        grid=(own,),
        in_specs=[pl.BlockSpec((1, depth, virtuals), lambda i: (i, 0, 0))],
        out_specs=pl.BlockSpec((1, virtuals, depth), lambda i: (i, 0, 0)),
        out_shape=jax.ShapeDtypeStruct((own, virtuals, depth), jnp.float32),
        cost_estimate=pl.CostEstimate(flops=0, bytes_accessed=8 * x.size, transcendentals=0),
        name="flip",
    )(x)


def split(x):
    high = x.astype(jnp.bfloat16)
    return high, (x - high.astype(jnp.float32)).astype(jnp.bfloat16)


def prep_kernel(x_ref, high_ref, low_ref):
    x = jnp.swapaxes(x_ref[...], 0, 1)
    x = x.reshape(high_ref.shape)
    high_ref[...], low_ref[...] = split(x)


def prep(x):
    occupied, virtuals, depth = x.shape
    rows = occupied * virtuals
    spec = pl.BlockSpec((8 * occupied, depth), lambda j: (j, 0))
    shape = jax.ShapeDtypeStruct((rows, depth), jnp.bfloat16)
    return pl.pallas_call(
        prep_kernel,
        grid=(virtuals // 8,),
        in_specs=[pl.BlockSpec((occupied, 8, depth), lambda j: (0, j, 0))],
        out_specs=[spec, spec],
        out_shape=[shape, shape],
        cost_estimate=pl.CostEstimate(flops=0, bytes_accessed=8 * x.size, transcendentals=0),
        name="prep",
    )(x)


def product_kernel(parts, aliased, where_ref, *refs):
    pieces, refs = refs[:parts], refs[parts:]
    high_ref, low_ref, row_ref, col_ref = refs[:4]
    out_ref, w_ref = refs[4 + aliased:]
    depth = pieces[0].shape[0]
    whole = parts * depth

    @pl.when(pl.program_id(0) == 0)
    def _():
        for j, piece in enumerate(pieces):
            block = lax.rem(where_ref[0] + parts - j, parts)
            start = pl.multiple_of(block * depth, depth)
            w_high, w_low = split(piece[...])
            w_ref[pl.ds(start, depth), :] = w_high
            w_ref[pl.ds(start + whole, depth), :] = w_high
            w_ref[pl.ds(start + 2 * whole, depth), :] = w_low

    high = high_ref[...]
    terms = jnp.concatenate([high, low_ref[...], high], axis=1)
    total = jnp.dot(terms, w_ref[...], preferred_element_type=jnp.float32)
    out_ref[...] = total / (row_ref[...] + col_ref[...])


def product(where, pieces, high, low, row_gap, col_gap, out, shape, start):
    parts = len(pieces)
    depth, width = pieces[0].shape
    rows, whole = high.shape
    tile = min(512, rows)
    chunk = start // width
    aliased = 0 if out is None else 1
    in_specs = [pl.BlockSpec((depth, width), lambda m, s: (0, 0), pipeline_mode=pl.Buffered(1))] * parts
    in_specs += [pl.BlockSpec((tile, whole), lambda m, s: (m, 0))] * 2
    in_specs += [pl.BlockSpec((tile, 1), lambda m, s: (m, 0))]
    in_specs += [pl.BlockSpec((1, width), lambda m, s: (0, chunk))]
    operands = [where, *pieces, high, low, row_gap, col_gap]
    if aliased:
        in_specs += [pl.BlockSpec(memory_space=pl.ANY)]
        operands += [out]
    return pl.pallas_call(
        lambda *refs: product_kernel(parts, aliased, *refs),
        grid_spec=pltpu.PrefetchScalarGridSpec(
            num_scalar_prefetch=1,
            grid=(rows // tile,),
            in_specs=in_specs,
            out_specs=pl.BlockSpec((tile, width), lambda m, s: (m, chunk)),
            scratch_shapes=[pltpu.VMEM((3 * whole, width), jnp.bfloat16)],
        ),
        out_shape=jax.ShapeDtypeStruct(shape, jnp.float32),
        input_output_aliases={len(operands) - 1: 0} if aliased else {},
        cost_estimate=pl.CostEstimate(
            flops=6 * rows * width * whole, bytes_accessed=4 * rows * (width + whole), transcendentals=0
        ),
        name="product",
    )(*operands)


def body(amplitudes, integrals, occ_energy, vir_energy):
    virtuals, own = amplitudes.shape[:2]
    occupied = own * lax.axis_size("row")
    whole = amplitudes.shape[2] * amplitudes.shape[3]
    columns = integrals.shape[1]
    parts = lax.axis_size("col")
    height = virtuals * occupied
    ring = [(j, (j + 1) % parts) for j in range(parts)]

    turned = jnp.transpose(amplitudes, (1, 2, 3, 0)).reshape(own, whole, virtuals)
    gathered = lax.all_gather(flip(turned), "row", axis=0, tiled=True)

    starts = [columns * cut // CUTS[-1] for cut in CUTS]
    chunks = []
    for c, (start, stop) in enumerate(zip(starts, starts[1:])):
        piece = integrals[:, start:stop]
        if c >= 2:
            piece, _ = lax.optimization_barrier((piece, chunks[c - 1][-2]))
        pieces = [piece]
        for _ in range(parts - 1):
            pieces.append(lax.ppermute(pieces[-1], "col", ring))
        chunks.append(pieces)

    row_vir = lax.dynamic_slice_in_dim(vir_energy, lax.axis_index("col") * virtuals, virtuals)
    row_gap = (row_vir[:, None] - occ_energy[None, :]).reshape(height, 1)
    col_virtuals = columns // occupied
    col_vir = lax.dynamic_slice_in_dim(vir_energy, lax.axis_index("row") * col_virtuals, col_virtuals)
    col_gap = (col_vir[:, None] - occ_energy[None, :]).reshape(1, columns)

    where = lax.axis_index("col").astype(jnp.int32).reshape(1)
    high, low = prep(gathered)
    out = None
    for start, pieces in zip(starts, chunks):
        out = product(where, pieces, high, low, row_gap, col_gap, out, (height, columns), start)
    return out


def solution(mesh):
    in_specs = (P("col", "row", None, None), P("col", "row"), P(), P())
    out_specs = P("col", "row")
    return jax.shard_map(body, mesh=mesh, in_specs=in_specs, out_specs=out_specs, check_vma=False)
```
